256 devices in a mesh: state: 64 (over x, y, z_lo), horizon: 4 (over z_hi, core).
Axes of the slice: x: 4, y: 4, z: 8 (z_hi: 2, z_lo: 4; z = z_hi * 4 + z_lo), core: 2. Of those that a mesh axis runs over, the one named last changes fastest.
Arguments:
- expect: bfloat16 [512, 2097152], P('horizon', 'state'), may hold values from -0.00018310547 to 0.00018310547
- steady_dist: float32 [2097152], P('state'), may hold values from 0.2 to 2
- policy_deriv: bfloat16 [128, 2097152], P('horizon', 'state'), may hold values from -16 to 16
- lottery_index: int32 [1024, 2048], P('state'), may hold values from 0 to 2046, as said below
- type_trans: float32 [16, 16], replicated, may hold values from 0.1 to 1
- migration: bfloat16 [64, 2, 16], P('state'), may hold values from 0.049804688 to 0.29882812
- discount: float32 [512], P('horizon'), may hold values from 0.3 to 1
Outputs:
- jacobian: float32 [128, 512], P('state', 'horizon')
- present_value: float32 [128, 512], P('state', 'horizon')
The draws below stay inside these ranges and needn't reach their ends.
Inputs may be any that keep to these rules, and one draw needn't show every extreme that they name: `lottery_index`: for every row and every block of 128 asset nodes, every index of the block lies between 128 * (m // 128) and 128 * (m // 128) + 254, where m is the block's smallest index.
All inputs are finite; a program needn't handle non-finite values.
Results may differ from the reference program's by a relative error of at most 0.0072.
Values may be sent and summed in bfloat16 or wider, within the bound.
A program may use at most 128 MiB of HBM per device.

```python
import math
import jax
import jax.numpy as jnp
from jax import lax

ASSETS = 2048
COLS = 128
TYPES = 16
STATES_DEV = 32768
REGIONS = 64
RESPONSE_PERIODS = 512
N_STATE = 64


def draw_lottery_index(key, part):
    base_key = jax.random.fold_in(key, 11)
    band_key, node_random_key = jax.random.split(base_key)
    blocks = ASSETS // 128
    row_count = REGIONS * TYPES
    block_ids = jnp.arange(blocks, dtype=jnp.int32)[None, :]
    starts = jnp.clip(block_ids + jax.random.randint(band_key, (row_count, blocks), -1, 1), 0, blocks - 2)
    offsets = jax.random.randint(node_random_key, (row_count, blocks, 128), 0, 255)
    offsets = offsets.at[:, :, 0].set(0).at[:, :, 1].set(254)
    return (128 * starts[:, :, None] + offsets).reshape(row_count, ASSETS).astype(jnp.int32)


def draw_discount(key, part):
    base_key = jax.random.fold_in(key, 23)
    rate_key, where_key, size_key = jax.random.split(base_key, 3)
    switching_intensities = jax.random.uniform(rate_key, (RESPONSE_PERIODS,), minval=0.0, maxval=2.0 / RESPONSE_PERIODS)
    wealth_points = jax.random.randint(where_key, (3,), 0, RESPONSE_PERIODS)
    patience_betas = jax.random.uniform(size_key, (3,), minval=0.5, maxval=0.8)
    impulse_pulses = jnp.ones((RESPONSE_PERIODS,), jnp.float32).at[wealth_points].multiply(patience_betas)
    return (jnp.exp(-switching_intensities) * impulse_pulses).astype(jnp.float32)


def raised(entries, own_key, source, target, parts, factor):
    def block_of(position):
        return (jnp.arange(entries.shape[position]) // (entries.shape[position] // parts)).reshape((-1,) + (1,) * (entries.ndim - 1 - position))

    first = jax.random.permutation(own_key, parts)[block_of(target)]
    other_side = (block_of(target) + parts // 2) % parts
    return jnp.where((block_of(source) == first) | (block_of(source) == other_side), factor * entries, entries)


def steps_of(own_key, shape, cuts, least, high):
    def one(axis_at, parts):
        heights = jax.random.uniform(jax.random.fold_in(jax.random.fold_in(own_key, 6), axis_at), (parts,), jnp.float32, least / len(cuts), high / len(cuts))
        return jnp.repeat(jnp.exp(heights), shape[axis_at] // parts).reshape((-1,) + (1,) * (len(shape) - axis_at - 1))

    level = one(*cuts[0])
    for cut in cuts[1:]:
        level = level * one(*cut)
    return level


def noise(key, dims, scale, reach, shards=(), held_as=jnp.bfloat16):
    factor_of = steps_of(key, dims, shards, -0.22, 0.18) if shards else 1.0
    drawn = jax.random.normal(key, dims, jnp.float32) * scale * factor_of
    return jnp.minimum(jnp.maximum(drawn, -reach), reach).astype(held_as)


def bell_draw_with(rng, dims, deviation, limit, pieces, heavy, kind=jnp.bfloat16):
    values = deviation * jax.random.normal(rng, dims, jnp.float32)
    if pieces:
        values = values * steps_of(rng, dims, pieces, -0.22, 0.18)
    return jnp.clip(raised(values, jax.random.fold_in(rng, 3), *heavy), -limit, limit).astype(kind)


def setup_inputs(seed: int = 0) -> dict:
    key_of = jax.random.split(jax.random.key(seed), 8)
    expect = noise(key_of[0], (RESPONSE_PERIODS, REGIONS * STATES_DEV), (512 * STATES_DEV * N_STATE) ** -0.5, 0.00018310547, ((0, 4), (1, 64)))
    steady_dist = jnp.clip(jnp.exp(math.log(2.0) - 2.3025851 * jax.random.uniform(key_of[1], (REGIONS * STATES_DEV,), jnp.float32) ** steps_of(key_of[1], (REGIONS * STATES_DEV,), ((0, 64),), -0.2, 0.2)), 0.2, 2.0)
    policy_deriv = bell_draw_with(key_of[2], (COLS, REGIONS * STATES_DEV), 1.0, 16.0, ((0, 4), (1, 64)), (1, 0, 64, 4.0))
    lottery_index = draw_lottery_index(jax.random.fold_in(key_of[7], 71), 0)
    type_trans = jnp.clip(jnp.exp(jax.random.uniform(key_of[4], (TYPES, TYPES), jnp.float32, math.log(0.1), math.log(1.0))), 0.1, 1.0)
    migration = jnp.clip(0.049804688 + 0.24902344 * jax.random.uniform(key_of[5], (REGIONS, 2, TYPES), jnp.float32) ** steps_of(key_of[5], (REGIONS, 2, TYPES), ((0, 64),), -0.2, 0.2), 0.049804688, 0.29882812).astype(jnp.bfloat16)
    discount = draw_discount(jax.random.fold_in(key_of[7], 71), 0)
    return dict(expect=expect, steady_dist=steady_dist, policy_deriv=policy_deriv, lottery_index=lottery_index, type_trans=type_trans, migration=migration, discount=discount)


def region_shift(policy_cols, steady_cols, lottery_rows, type_mix):
    num_cols = policy_cols.shape[0]
    household_type_count = lottery_rows.shape[0]
    num_assets = lottery_rows.shape[1]
    rounded = (steady_cols[None, :] * policy_cols.astype(jnp.float32)).astype(jnp.bfloat16)
    rounded = lax.optimization_barrier(rounded)
    weights = rounded.astype(jnp.float32).reshape(num_cols, household_type_count, num_assets)
    type_rows = lax.broadcasted_iota(jnp.int32, (household_type_count, num_assets), 0)
    landed = jnp.zeros((num_cols, household_type_count, num_assets), jnp.float32)
    landed = landed.at[:, type_rows, lottery_rows].add(weights)
    landed = landed.at[:, type_rows, lottery_rows + 1].add(-weights)
    blended = jnp.einsum("cxa,xy->cya", landed, type_mix, precision=lax.Precision.HIGHEST)
    return blended.reshape(num_cols, household_type_count * num_assets).astype(jnp.bfloat16)


def weigh(entering_lines, switching_intensities):
    height = entering_lines.shape[0]
    scaled = entering_lines.astype(jnp.float32).reshape(height, switching_intensities.shape[0], -1) * switching_intensities[None, :, None]
    return scaled.reshape(height, -1).astype(jnp.bfloat16)


def reference(expect, steady_dist, policy_deriv, lottery_index, type_trans, migration, discount):
    regions = migration.shape[0]
    horizons = expect.shape[0]
    type_mix = type_trans / jnp.sum(type_trans, axis=1, keepdims=True)
    all_rates = migration.astype(jnp.float32)

    def one_region(flow_sum, region):
        start = (region * STATES_DEV).astype(jnp.int32)
        shift_cols = region_shift(
            lax.dynamic_slice_in_dim(policy_deriv, start, STATES_DEV, 1),
            lax.dynamic_slice_in_dim(steady_dist, start, STATES_DEV, 0),
            lax.dynamic_slice_in_dim(lottery_index, (region * TYPES).astype(jnp.int32), TYPES, 0),
            type_mix)
        higher_begin = (((region + 1) % regions) * STATES_DEV).astype(jnp.int32)
        lower_start = (((region + regions - 1) % regions) * STATES_DEV).astype(jnp.int32)
        region_rates = lax.dynamic_index_in_dim(all_rates, region.astype(jnp.int32), 0, keepdims=False)
        stay_rates = 1.0 - region_rates[0] - region_rates[1]
        weighted = (
            weigh(lax.dynamic_slice_in_dim(expect, start, STATES_DEV, 1), stay_rates),
            weigh(lax.dynamic_slice_in_dim(expect, higher_begin, STATES_DEV, 1), region_rates[1]),
            weigh(lax.dynamic_slice_in_dim(expect, lower_start, STATES_DEV, 1), region_rates[0]),
        )
        for part_rows in weighted:
            flow_sum = flow_sum + jnp.dot(shift_cols, part_rows.T, preferred_element_type=jnp.float32)
        return flow_sum, None

    flow_total, _ = lax.scan(one_region, jnp.zeros((COLS, horizons), jnp.float32),
                             jnp.arange(regions, dtype=jnp.int32))

    def diagonal_row(previous, row_now):
        shifted = jnp.concatenate([jnp.zeros((1,), jnp.float32), previous[:-1]])
        current = row_now + shifted
        return current, current

    _, jacobian = lax.scan(diagonal_row, jnp.zeros((horizons,), jnp.float32), flow_total)

    def backward(carried_over, item):
        column_now, factor = item
        current = column_now + factor * carried_over
        return current, current

    _, values = lax.scan(backward, jnp.zeros((COLS,), jnp.float32), (jacobian.T, discount), reverse=True)
    return jacobian, values.T
```

```python
import jax
import jax.numpy as jnp
from jax import lax
from jax.experimental import pallas as pl
from jax.experimental.pallas import tpu as pltpu
from jax.sharding import PartitionSpec as P

MESH = pl.DeviceIdType.MESH
BLOCK = 128
CHUNKS = 8
PARTS = 4
STEPS = 5
ONE_HOP = STEPS + 1
NT = (((1,), (1,)), ((), ()))
bf = jnp.bfloat16
f32 = jnp.float32


def locate(index, offsets, keys):
    types = index.shape[0]
    blocks = offsets.shape[0]
    lane = lax.broadcasted_iota(jnp.int32, (types, 4*BLOCK), 1)
    acc = lane // (16*blocks) + 16 * (lane % 16)
    acc = acc.astype(f32)
    for k in range(blocks):
        nodes = index[:, k*BLOCK:(k+1)*BLOCK]
        base = lax.shift_right_logical(jnp.min(nodes, axis=1, keepdims=True), 7)
        away = (nodes - base * BLOCK).astype(f32)
        offsets[k] = away
        acc = acc + jnp.where((lane // 16) % blocks == k, base.astype(f32), 0.0)
    for q in range(4):
        keys[q] = acc[:, q*BLOCK:(q+1)*BLOCK]


def spread_mix(trans, kron):
    types = trans.shape[0]
    mix = trans[...] / jnp.sum(trans[...], axis=1, keepdims=True)
    high = mix.astype(bf)
    low = (mix - high.astype(f32)).astype(bf)
    wide = types*16
    tall = lax.broadcasted_iota(jnp.int32,(wide,types),0)//16 == lax.broadcasted_iota(jnp.int32,(wide,types),1)
    tall = jnp.where(tall,1.0,0.0).astype(bf)
    same = lax.broadcasted_iota(jnp.int32,(wide,wide),0)%16 == lax.broadcasted_iota(jnp.int32,(wide,wide),1)%16
    for n, part in enumerate((high, low)):
        left = lax.dot_general(tall, part, NT, preferred_element_type=f32)
        both = lax.dot_general(left.astype(bf), tall, NT, preferred_element_type=f32)
        kron[n*wide:(n+1)*wide, :] = jnp.where(same, both, 0.0).astype(bf)

def land_pieces(mass, offsets, keys, kron, moved, landed, out):
    types = keys.shape[1]
    blocks = offsets.shape[0]
    cols = mass.shape[0]
    assets = blocks * BLOCK
    wide = types * 16
    node = lax.broadcasted_iota(jnp.int32, (2 * BLOCK, BLOCK), 0).astype(f32).astype(bf)

    def halves(value):
        high = value.astype(bf)
        return high, (value - high.astype(f32)).astype(bf)

    def one_block(k):
        for x in range(types):
            lanes = pl.ds(pl.multiple_of(x * assets + k * BLOCK, BLOCK), BLOCK)
            away = offsets[k, x : x + 1, :]
            here, there = away.astype(bf), (away + 1.0).astype(bf)
            lottery = jnp.where(node == here, bf(1), jnp.where(node == there, bf(-1), bf(0)))
            got = lax.dot_general(mass[:, lanes], lottery, NT, preferred_element_type=f32)
            for n, part in enumerate(halves(got)):
                for h in range(2):
                    rows = pl.ds(pl.multiple_of(h * blocks * 16 + k * 16, 16), 16)
                    for g in range(cols // 16):
                        moved[n, x, rows, g * BLOCK : (g + 1) * BLOCK] = part[
                            g * 16 : (g + 1) * 16, h * BLOCK : (h + 1) * BLOCK
                        ]

    row = lax.broadcasted_iota(jnp.int32, (blocks * 16, 4 * BLOCK), 0)
    row_key = (row // 16 + 16 * (row % 16)).astype(f32).astype(bf)

    def one_type(x):
        key = jnp.concatenate([keys[q, pl.ds(x, 1), :] for q in range(4)], axis=1)
        place = jnp.where(row_key == key.astype(bf), bf(1), bf(0))
        total = jnp.dot(place, moved[0, x], preferred_element_type=f32)
        total += jnp.dot(place, moved[1, x], preferred_element_type=f32)
        rows = pl.ds(pl.multiple_of(x * 16, 16), 16)
        for n, part in enumerate(halves(total)):
            for b in range(blocks):
                for g in range(cols // 16):
                    landed[n, g, rows, b * BLOCK : (b + 1) * BLOCK] = part[
                        b * 16 : (b + 1) * 16, g * BLOCK : (g + 1) * BLOCK
                    ]

    tile = 256

    def blend(n):
        lanes = pl.ds(pl.multiple_of(n * tile, tile), tile)
        for g in range(cols // 16):
            both = jnp.dot(kron[...], landed[0, g, :, lanes], preferred_element_type=f32)
            rest = jnp.dot(kron[0:wide, :], landed[1, g, :, lanes], preferred_element_type=f32)
            total = (both[:wide] + both[wide:] + rest).astype(bf)
            for y in range(types):
                out[y * cols + g * 16 : y * cols + g * 16 + 16, lanes] = total[
                    y * 16 : (y + 1) * 16
                ]

    return (blocks, one_block), (types, one_type), (assets // tile, blend)


def flow_kernel(
    expect_in, policy_in, steady_in, index_in, trans_in, migration_in, discount_in, jac_out, value_out,
    lines, held, flow, half, pairs, from_plane, from_line, betas, wide, powers,
    mass, raw, steady, nodes, short, trans, moves, rates, weights, offsets, keys, kron, moved, landed, discount,
    local_sem, send_sem, recv_sem, last_sem, tail_send, tail_recv,
):
    state, horizon = lax.axis_index("state"), lax.axis_index("horizon")
    core, upper, low = horizon % 2, horizon // 2, state % 4
    z = upper * 4 + low
    way = 1 - 2 * core
    rows_all, assets = held.shape[1:]
    types = trans.shape[0]
    cols = rows_all // types
    chunk_rows = rows_all // CHUNKS
    chunk_types = types // CHUNKS
    shifts = {1: 1, 3: -1, 4: 0, 5: 1}

    def origin(step):
        z0 = (z - way * step + 40) % 8
        if step == 0:
            return state, z0
        if step == 2:
            return state - low + z0 % 4, z0
        return (state - way * shifts[step] + 64) % 64, z0

    def place(region, z0, step):
        at = (z0 + way * step + 40) % 8
        if step == 2:
            there = region - region % 4 + at % 4
        else:
            there = (region + way * shifts[step] + 64) % 64
        return there, (at // 4) * 2 + core

    def target(step):
        return place(*origin(step - 1), step)

    def source(step):
        region, z0 = origin(step)
        return place(region, z0, step - 1) if step > 1 else (region, (z0 // 4) * 2 + core)

    hop_to = ((state - way + 64) % 64, ((z - way + 8) % 8 // 4) * 2 + core)
    hop_from = ((state + way + 64) % 64, ((z + way + 8) % 8 // 4) * 2 + core)
    other = (state, horizon + way)
    ahead = ((state + 1) % 64, ((z + 1) % 8 // 4) * 2 + core)
    behind = ((state + 63) % 64, ((z + 7) % 8 // 4) * 2 + core)
    column = state // 4

    def plane_at(dx, dy):
        return ((column // 4 + dx) % 4) * 4 + (column + dy) % 4

    def plane_peer(dx, dy):
        return (plane_at(dx, dy) * 4 + low, horizon)

    def line_peer(dz, flip):
        at = (z + dz) % 8
        return (state - low + at % 4, (at // 4) * 2 + core + flip * way)

    def mate(dh):
        return (state, (horizon + dh) % 4)

    far = (2, 1, 3, 0)
    plane_turns = sorted(
        [(dx, dy) for dx in far for dy in far if dx or dy], key=lambda t: far.index(t[0]) + far.index(t[1])
    )
    line_turns = [(dz, flip) for dz in (4, 3, 5, 2, 6, 1, 7, 0) for flip in (0, 1) if dz or flip]
    span = assets * types // PARTS

    def part(n):
        return pl.ds(n * span, span)

    loads = [
        pltpu.make_async_copy(src, dst, local_sem.at[n])
        for n, (src, dst) in enumerate(
            [
                (steady_in, steady),
                (migration_in, moves),
                (index_in, nodes),
                (discount_in, discount),
                (trans_in, trans),
                (expect_in, lines.at[core]),
            ]
            + [(policy_in.at[:, part(n)], mass.at[:, part(n)]) for n in range(PARTS)]
        )
    ]
    for load in loads[:5] + loads[6:] + loads[5:6]:
        load.start()
    barrier = pltpu.get_barrier_semaphore()
    greeted = [source(step) for step in range(1, STEPS + 1)] + [hop_from, other, ahead, behind]
    greeted += [plane_peer(-dx % 4, -dy % 4) for dx, dy in plane_turns]
    greeted += [line_peer(-dz % 8, flip) for dz, flip in line_turns]
    for peer in greeted:
        pl.semaphore_signal(barrier, inc=1, device_id=peer, device_id_type=MESH)

    for load in loads[:5]:
        load.wait()
    short[0] = nodes[...].astype(jnp.int16)
    rates[0] = jnp.zeros((8, BLOCK), f32)
    rates[0, 0:2, 0:types] = moves[...].astype(f32)
    each = assets // BLOCK

    def weigh(x, carry):
        for n in range(each):
            lanes = pl.ds(pl.multiple_of(x * assets + n * BLOCK, BLOCK), BLOCK)
            factor = steady[pl.ds(x * each + n, 1), :]
            mass[:, lanes] = (factor * mass[:, lanes].astype(f32)).astype(bf)
        return carry

    def chunk(c):
        return pl.ds(pl.multiple_of(c * chunk_rows, chunk_rows), chunk_rows)

    def move(step, c):
        return pltpu.make_async_remote_copy(
            src_ref=held.at[step - 1, chunk(c)],
            dst_ref=held.at[step, chunk(c)],
            send_sem=send_sem.at[step],
            recv_sem=recv_sem.at[step, c],
            device_id=target(step),
            device_id_type=MESH,
        )

    def last_move(y):
        rows = pl.ds(pl.multiple_of(y * cols, cols), cols)
        return pltpu.make_async_remote_copy(
            src_ref=held.at[STEPS - 1, rows],
            dst_ref=held.at[STEPS, rows],
            send_sem=send_sem.at[STEPS],
            recv_sem=last_sem.at[y],
            device_id=target(STEPS),
            device_id_type=MESH,
        )

    def across(src, dst, n, to):
        return pltpu.make_async_remote_copy(
            src_ref=src,
            dst_ref=dst,
            send_sem=tail_send.at[28 + n],
            recv_sem=tail_recv.at[28 + n],
            device_id=to,
            device_id_type=MESH,
        )

    early_moves = [
        across(rates.at[0], rates.at[1], 0, ahead),
        across(short.at[0], short.at[1], 1, hop_to),
        across(rates.at[0], rates.at[2], 2, behind),
        across(expect_in, lines.at[core], 3, other),
    ]
    lines_landed = across(expect_in, lines.at[1 - core], 3, other)
    raw_moves = [
        across(mass.at[:, part(n)], raw.at[:, part(n)], 4 + n, hop_to) for n in range(PARTS)
    ]
    for n in range(PARTS):
        loads[6 + n].wait()
        lax.fori_loop(n * types // PARTS, (n + 1) * types // PARTS, weigh, 0)
        if n == 0:
            pl.semaphore_wait(barrier, len(greeted))
        raw_moves[n].start()
    for copy in early_moves:
        copy.start()

    def beta_move(dh):
        return pltpu.make_async_remote_copy(
            src_ref=discount,
            dst_ref=betas.at[horizon],
            send_sem=tail_send.at[24 + dh],
            recv_sem=tail_recv.at[24 + dh],
            device_id=mate(dh),
            device_id_type=MESH,
        )

    def loop(body):
        lax.fori_loop(0, CHUNKS, lambda c, carry: (body(c), carry)[1], 0)

    for dh in (1, 2, 3):
        beta_move(dh).start()
    betas[horizon] = discount[...]

    spread_mix(trans, kron)
    locate(nodes, offsets, keys)
    for count, piece in land_pieces(mass, offsets, keys, kron, moved, landed, held.at[0]):
        lax.fori_loop(0, count, lambda n, carry, piece=piece: (piece(n), carry)[1], 0)
    loop(lambda c: move(1, c).start())

    early_moves[0].wait_recv()
    early_moves[2].wait_recv()
    diagonal = lax.broadcasted_iota(jnp.int32, (types, BLOCK), 0) == lax.broadcasted_iota(
        jnp.int32, (types, BLOCK), 1
    )
    mine = 1.0 - rates[0, 0:1, :] - rates[0, 1:2, :]
    for n, line in enumerate((mine, rates[1, 1:2, :], rates[2, 0:1, :])):
        upright = jnp.sum(jnp.where(diagonal, line, 0.0), axis=1, keepdims=True)
        weights[n] = jnp.broadcast_to(upright, (types, BLOCK))

    for copy in raw_moves:
        copy.wait_recv()
    early_moves[1].wait_recv()
    nodes[...] = short[1].astype(jnp.int32)
    locate(nodes, offsets, keys)
    pieces = land_pieces(raw, offsets, keys, kron, moved, landed, held.at[ONE_HOP])

    for step in range(1, STEPS - 1):

        def onward(c, step=step):
            move(step, c).wait_recv()
            move(step + 1, c).start()
            count, piece = pieces[step - 1]
            for n in range(count // CHUNKS):
                piece(c * (count // CHUNKS) + n)

        loop(onward)

    mirror = low + core * (3 - 2 * low)
    edge_low, edge_high = (3 - mirror) // 3, mirror // 3
    edge = edge_low + edge_high

    def multiply(late, y):
        same = 4 * (1 - edge_low) if late else 4 * edge_low
        prior = STEPS if late else 1
        after = 3 + 3 * edge if late else 6 - 3 * edge
        rows = pl.ds(pl.multiple_of(y * cols, cols), cols)
        total = None
        for n, slot in ((0, same), (1 + core, prior), (2 - core, after)):
            weight = jnp.concatenate([weights[n, pl.ds(y, 1), :]] * (assets // BLOCK), axis=1)
            term = held[slot, rows, :].astype(f32) * weight
            total = term if total is None else total + term
        lanes = pl.ds(pl.multiple_of(y * assets, assets), assets)
        right = jnp.concatenate([lines[0, :, lanes], lines[1, :, lanes]], axis=0)
        high = total.astype(bf)
        left = jnp.concatenate([high, (total - high.astype(f32)).astype(bf)], axis=0)
        both = lax.dot_general(left, right, NT, preferred_element_type=f32)
        flow[late] += both[:cols] + both[cols:]

    def beta_landed(dh):
        return pltpu.make_async_remote_copy(
            src_ref=discount,
            dst_ref=betas.at[(horizon + 4 - dh) % 4],
            send_sem=tail_send.at[24 + dh],
            recv_sem=tail_recv.at[24 + dh],
            device_id=mate(dh),
            device_id_type=MESH,
        )

    for dh in (1, 2, 3):
        beta_landed(dh).wait_recv()
    length = 4 * BLOCK
    hops = length.bit_length() - 1
    ids = lax.broadcasted_iota(jnp.int32, (2, length), 1)
    factor = jnp.concatenate([betas[h] for h in range(4)], axis=1)
    factor = jnp.broadcast_to(factor, (2, length))
    for n in range(hops):
        powers[n] = factor
        lagged = pltpu.roll(factor, length - 2**n, 1)
        factor = factor * jnp.where(ids < length - 2**n, lagged, 0.0)

    loads[5].wait()
    lines_landed.wait_recv()
    flow[...] = jnp.zeros_like(flow)

    def early(c):
        move(STEPS - 1, c).wait_recv()
        for i in range(chunk_types):
            last_move(c * chunk_types + i).start()
        for i in range(chunk_types):
            multiply(0, c * chunk_types + i)

    loop(early)

    def late(y, carry):
        last_move(y).wait_recv()
        multiply(1, y)
        return carry

    lax.fori_loop(0, types, late, 0)

    late_half = upper + (1 - edge_low) * (1 - 2 * upper)
    half[...] = jnp.zeros_like(half)
    for when, at in ((0, 1 - late_half), (1, late_half)):
        rows = pl.ds(pl.multiple_of((at * 2 + core) * cols, cols), cols)
        half[rows, : 2 * BLOCK] = flow[when]
    total = half[...]
    rows_at = lax.broadcasted_iota(jnp.int32, total.shape, 0)
    offset = 1
    while offset < 4 * cols:
        lagged = pltpu.roll(pltpu.roll(total, offset, 0), offset, 1)
        total = total + jnp.where(rows_at >= offset, lagged, 0.0)
        offset *= 2
    half[...] = total

    def plane_move(n, dx, dy):
        block = pl.ds(pl.multiple_of(plane_at(dx, dy) * 8, 8), 8)
        return pltpu.make_async_remote_copy(
            src_ref=half.at[block],
            dst_ref=from_plane.at[n],
            send_sem=tail_send.at[0],
            recv_sem=tail_recv.at[0],
            device_id=plane_peer(dx, dy),
            device_id_type=MESH,
        )

    def plane_all():
        return pltpu.make_async_remote_copy(
            src_ref=half.at[pl.ds(0, 8 * len(plane_turns))],
            dst_ref=from_plane,
            send_sem=tail_send.at[0],
            recv_sem=tail_recv.at[0],
            device_id=plane_peer(1, 0),
            device_id_type=MESH,
        )

    for n, (dx, dy) in enumerate(plane_turns):
        plane_move(n, dx, dy).start()

    for step in range(1, STEPS + 1):
        pltpu.make_async_remote_copy(
            src_ref=held.at[step - 1],
            dst_ref=held.at[step],
            send_sem=send_sem.at[step],
            recv_sem=recv_sem.at[1, 0],
            device_id=target(step),
            device_id_type=MESH,
        ).wait_send()
    for copy in early_moves + raw_moves:
        copy.wait_send()
    for k in (1, 2, 3):
        beta_move(k).wait_send()

    plane_all().wait_recv()
    parts = [half[pl.ds(pl.multiple_of(column * 8, 8), 8), :]]
    parts += [from_plane[n] for n in range(15)]
    while len(parts) > 1:
        parts = [a + b for a, b in zip(parts[::2], parts[1::2])]
    for q in range(4):
        pairs[q] = parts[0][2 * q : 2 * q + 2]
    here = z * 2 + core

    def line_move(dz, flip):
        return pltpu.make_async_remote_copy(
            src_ref=pairs.at[(low + dz) % 4],
            dst_ref=from_line.at[here],
            send_sem=tail_send.at[1],
            recv_sem=tail_recv.at[1],
            device_id=line_peer(dz, flip),
            device_id_type=MESH,
        )

    def line_all():
        return pltpu.make_async_remote_copy(
            src_ref=from_line.at[pl.ds(0, len(line_turns))],
            dst_ref=from_line.at[pl.ds(0, len(line_turns))],
            send_sem=tail_send.at[1],
            recv_sem=tail_recv.at[1],
            device_id=line_peer(1, 0),
            device_id_type=MESH,
        )

    for dz, flip in line_turns:
        line_move(dz, flip).start()
    from_line[here] = pairs[low]

    line_all().wait_recv()

    sums = []
    for n in range(2):
        parts = [from_line[8 * n + q] for q in range(8)]
        while len(parts) > 1:
            parts = [a + b for a, b in zip(parts[::2], parts[1::2])]
        sums.append(parts[0])
    jac = jnp.concatenate(
        [
            sums[0][:, : 2 * BLOCK],
            sums[1][:, :BLOCK] + sums[0][:, 2 * BLOCK :],
            sums[1][:, BLOCK : 2 * BLOCK],
        ],
        axis=1,
    )
    value = jac
    for n in range(hops):
        lagged = pltpu.roll(value, length - 2**n, 1)
        value = value + powers[n] * jnp.where(ids < length - 2**n, lagged, 0.0)
    wide[0] = jac
    wide[1] = value
    lanes = pl.ds(pl.multiple_of(horizon * BLOCK, BLOCK), BLOCK)
    jac_out[...] = wide[0, :, lanes]
    value_out[...] = wide[1, :, lanes]
    plane_all().wait_send()
    line_all().wait_send()


def local(expect, steady_dist, policy_deriv, lottery_index, type_trans, migration, discount):
    types, assets = lottery_index.shape
    cols, states = policy_deriv.shape
    count = expect.shape[0]
    far = pl.BlockSpec(memory_space=pltpu.HBM)
    vmem = pl.BlockSpec(memory_space=pltpu.VMEM)
    return pl.pallas_call(
        flow_kernel,
        out_shape=[jax.ShapeDtypeStruct((2, count), f32)] * 2,
        in_specs=[far] * 7,
        out_specs=[vmem, vmem],
        scratch_shapes=[
            pltpu.VMEM((2, count, states), bf),
            pltpu.VMEM((ONE_HOP + 1, types * cols, assets), bf),
            pltpu.VMEM((2, cols, 2 * count), f32),
            pltpu.VMEM((4 * cols, 3 * BLOCK), f32),
            pltpu.VMEM((4, 2, 3 * BLOCK), f32),
            pltpu.VMEM((15, 8, 3 * BLOCK), f32),
            pltpu.VMEM((16, 2, 3 * BLOCK), f32),
            pltpu.VMEM((4, 1, count), f32),
            pltpu.VMEM((2, 2, 4 * BLOCK), f32),
            pltpu.VMEM((9, 2, 4 * BLOCK), f32),
            pltpu.VMEM((cols, states), bf),
            pltpu.VMEM((cols, states), bf),
            pltpu.VMEM((states // BLOCK, BLOCK), f32),
            pltpu.VMEM((types, assets), jnp.int32),
            pltpu.VMEM((2, types, assets), jnp.int16),
            pltpu.VMEM((types, types), f32),
            pltpu.VMEM((2, types), bf),
            pltpu.VMEM((3, 8, BLOCK), f32),
            pltpu.VMEM((3, types, BLOCK), f32),
            pltpu.VMEM((assets // BLOCK, types, BLOCK), f32),
            pltpu.VMEM((4, types, BLOCK), f32),
            pltpu.VMEM((2 * types * 16, types * 16), bf),
            pltpu.VMEM((2, types, 32 * assets // BLOCK, 2 * BLOCK), bf),
            pltpu.VMEM((2, 2, types * 16, assets), bf),
            pltpu.VMEM((1, count), f32),
            pltpu.SemaphoreType.DMA((6 + PARTS,)),
            pltpu.SemaphoreType.DMA((STEPS + 1,)),
            pltpu.SemaphoreType.DMA((STEPS + 1, CHUNKS)),
            pltpu.SemaphoreType.DMA((types,)),
            pltpu.SemaphoreType.DMA((48 + PARTS,)),
            pltpu.SemaphoreType.DMA((48 + PARTS,)),
        ],
        compiler_params=pltpu.CompilerParams(
            collective_id=0, has_side_effects=True, vmem_limit_bytes=52 * 2**20
        ),
        name="flow",
    )(
        *[
            pltpu.with_memory_space_constraint(value, pltpu.HBM)
            for value in (
                expect,
                policy_deriv,
                steady_dist.reshape(-1, BLOCK),
                lottery_index,
                type_trans,
                migration.reshape(2, types),
                discount.reshape(1, count),
            )
        ]
    )


def solution(mesh):
    return jax.shard_map(
        local,
        mesh=mesh,
        in_specs=(
            P("horizon", "state"),
            P("state"),
            P("horizon", "state"),
            P("state", None),
            P(),
            P("state", None, None),
            P("horizon"),
        ),
        out_specs=(P("state", "horizon"), P("state", "horizon")),
        check_vma=False,
    )
```

```python
import jax
import jax.numpy as jnp
from jax import lax
from jax.experimental import pallas as pl
from jax.experimental.pallas import tpu as pltpu
from jax.sharding import PartitionSpec as P

MESH = pl.DeviceIdType.MESH
BLOCK = 128
CHUNKS = 8
PARTS = 4
STEPS = 5
ONE_HOP = STEPS + 1
NT = (((1,), (1,)), ((), ()))
bf = jnp.bfloat16
f32 = jnp.float32


def locate(index, offsets, keys):
    types = index.shape[0]
    blocks = offsets.shape[0]
    lane = lax.broadcasted_iota(jnp.int32, (types, 4*BLOCK), 1)
    acc = lane // (16*blocks) + 16 * (lane % 16)
    acc = acc.astype(f32)
    for k in range(blocks):
        nodes = index[:, k*BLOCK:(k+1)*BLOCK]
        base = lax.shift_right_logical(jnp.min(nodes, axis=1, keepdims=True), 7)
        away = (nodes - base * BLOCK).astype(f32)
        offsets[k] = away
        acc = acc + jnp.where((lane // 16) % blocks == k, base.astype(f32), 0.0)
    for q in range(4):
        keys[q] = acc[:, q*BLOCK:(q+1)*BLOCK]


def spread_mix(trans, kron):
    types = trans.shape[0]
    mix = trans[...] / jnp.sum(trans[...], axis=1, keepdims=True)
    high = mix.astype(bf)
    low = (mix - high.astype(f32)).astype(bf)
    wide = types*16
    tall = lax.broadcasted_iota(jnp.int32,(wide,types),0)//16 == lax.broadcasted_iota(jnp.int32,(wide,types),1)
    tall = jnp.where(tall,1.0,0.0).astype(bf)
    same = lax.broadcasted_iota(jnp.int32,(wide,wide),0)%16 == lax.broadcasted_iota(jnp.int32,(wide,wide),1)%16
    for n, part in enumerate((high, low)):
        left = lax.dot_general(tall, part, NT, preferred_element_type=f32)
        both = lax.dot_general(left.astype(bf), tall, NT, preferred_element_type=f32)
        kron[n*wide:(n+1)*wide, :] = jnp.where(same, both, 0.0).astype(bf)

def land_pieces(mass, offsets, keys, kron, moved, landed, out):
    types = keys.shape[1]
    blocks = offsets.shape[0]
    cols = mass.shape[0]
    assets = blocks * BLOCK
    wide = types * 16
    node = lax.broadcasted_iota(jnp.int32, (2 * BLOCK, BLOCK), 0).astype(f32).astype(bf)

    def halves(value):
        high = value.astype(bf)
        return high, (value - high.astype(f32)).astype(bf)

    def one_block(k):
        for x in range(types):
            lanes = pl.ds(pl.multiple_of(x * assets + k * BLOCK, BLOCK), BLOCK)
            away = offsets[k, x : x + 1, :]
            here, there = away.astype(bf), (away + 1.0).astype(bf)
            lottery = jnp.where(node == here, bf(1), jnp.where(node == there, bf(-1), bf(0)))
            got = lax.dot_general(mass[:, lanes], lottery, NT, preferred_element_type=f32)
            for n, part in enumerate(halves(got)):
                for h in range(2):
                    rows = pl.ds(pl.multiple_of(h * blocks * 16 + k * 16, 16), 16)
                    for g in range(cols // 16):
                        moved[n, x, rows, g * BLOCK : (g + 1) * BLOCK] = part[
                            g * 16 : (g + 1) * 16, h * BLOCK : (h + 1) * BLOCK
                        ]

    row = lax.broadcasted_iota(jnp.int32, (blocks * 16, 4 * BLOCK), 0)
    row_key = (row // 16 + 16 * (row % 16)).astype(f32).astype(bf)

    def one_type(x):
        key = jnp.concatenate([keys[q, pl.ds(x, 1), :] for q in range(4)], axis=1)
        place = jnp.where(row_key == key.astype(bf), bf(1), bf(0))
        total = jnp.dot(place, moved[0, x], preferred_element_type=f32)
        total += jnp.dot(place, moved[1, x], preferred_element_type=f32)
        rows = pl.ds(pl.multiple_of(x * 16, 16), 16)
        for n, part in enumerate(halves(total)):
            for b in range(blocks):
                for g in range(cols // 16):
                    landed[n, g, rows, b * BLOCK : (b + 1) * BLOCK] = part[
                        b * 16 : (b + 1) * 16, g * BLOCK : (g + 1) * BLOCK
                    ]

    tile = 256

    def blend(n):
        lanes = pl.ds(pl.multiple_of(n * tile, tile), tile)
        for g in range(cols // 16):
            both = jnp.dot(kron[...], landed[0, g, :, lanes], preferred_element_type=f32)
            rest = jnp.dot(kron[0:wide, :], landed[1, g, :, lanes], preferred_element_type=f32)
            total = (both[:wide] + both[wide:] + rest).astype(bf)
            for y in range(types):
                out[y * cols + g * 16 : y * cols + g * 16 + 16, lanes] = total[
                    y * 16 : (y + 1) * 16
                ]

    return (blocks, one_block), (types, one_type), (assets // tile, blend)


def flow_kernel(
    expect_in, policy_in, steady_in, index_in, trans_in, migration_in, discount_in, out,
    lines, held, flow, half, pairs, from_plane, from_line, betas, wide, powers,
    mass, raw, steady, nodes, short, trans, moves, rates, weights, offsets, keys, kron, moved, landed, discount,
    local_sem, send_sem, recv_sem, last_sem, tail_send, tail_recv,
):
    state, horizon = lax.axis_index("state"), lax.axis_index("horizon")
    core, upper, low = horizon % 2, horizon // 2, state % 4
    z = upper * 4 + low
    way = 1 - 2 * core
    rows_all, assets = held.shape[1:]
    types = trans.shape[0]
    cols = rows_all // types
    chunk_rows = rows_all // CHUNKS
    chunk_types = types // CHUNKS
    shifts = {1: 1, 3: -1, 4: 0, 5: 1}

    def origin(step):
        z0 = (z - way * step + 40) % 8
        if step == 0:
            return state, z0
        if step == 2:
            return state - low + z0 % 4, z0
        return (state - way * shifts[step] + 64) % 64, z0

    def place(region, z0, step):
        at = (z0 + way * step + 40) % 8
        if step == 2:
            there = region - region % 4 + at % 4
        else:
            there = (region + way * shifts[step] + 64) % 64
        return there, (at // 4) * 2 + core

    def target(step):
        return place(*origin(step - 1), step)

    def source(step):
        region, z0 = origin(step)
        return place(region, z0, step - 1) if step > 1 else (region, (z0 // 4) * 2 + core)

    hop_to = ((state - way + 64) % 64, ((z - way + 8) % 8 // 4) * 2 + core)
    hop_from = ((state + way + 64) % 64, ((z + way + 8) % 8 // 4) * 2 + core)
    other = (state, horizon + way)
    ahead = ((state + 1) % 64, ((z + 1) % 8 // 4) * 2 + core)
    behind = ((state + 63) % 64, ((z + 7) % 8 // 4) * 2 + core)
    column = state // 4

    def plane_at(dx, dy):
        return ((column // 4 + dx) % 4) * 4 + (column + dy) % 4

    def plane_peer(dx, dy):
        return (plane_at(dx, dy) * 4 + low, horizon)

    def line_peer(dz, flip):
        at = (z + dz) % 8
        return (state - low + at % 4, (at // 4) * 2 + core + flip * way)

    def mate(dh):
        return (state, (horizon + dh) % 4)

    far = (2, 1, 3, 0)
    plane_turns = sorted(
        [(dx, dy) for dx in far for dy in far if dx or dy], key=lambda t: far.index(t[0]) + far.index(t[1])
    )
    line_turns = [(dz, flip) for dz in (4, 3, 5, 2, 6, 1, 7, 0) for flip in (0, 1) if dz or flip]
    span = assets * types // PARTS

    def part(n):
        return pl.ds(n * span, span)

    loads = [
        pltpu.make_async_copy(src, dst, local_sem.at[n])
        for n, (src, dst) in enumerate(
            [
                (steady_in, steady),
                (migration_in, moves),
                (index_in, nodes),
                (discount_in, discount),
                (trans_in, trans),
                (expect_in, lines.at[core]),
            ]
            + [(policy_in.at[:, part(n)], mass.at[:, part(n)]) for n in range(PARTS)]
        )
    ]
    for load in loads[:5] + loads[6:] + loads[5:6]:
        load.start()
    barrier = pltpu.get_barrier_semaphore()
    greeted = [source(step) for step in range(1, STEPS + 1)] + [hop_from, other, ahead, behind]
    greeted += [plane_peer(-dx % 4, -dy % 4) for dx, dy in plane_turns]
    greeted += [line_peer(-dz % 8, flip) for dz, flip in line_turns]
    for peer in greeted:
        pl.semaphore_signal(barrier, inc=1, device_id=peer, device_id_type=MESH)

    for load in loads[:5]:
        load.wait()
    short[0] = nodes[...].astype(jnp.int16)
    rates[0] = jnp.zeros((8, BLOCK), f32)
    rates[0, 0:2, 0:types] = moves[...].astype(f32)
    each = assets // BLOCK

    def weigh(x, carry):
        for n in range(each):
            lanes = pl.ds(pl.multiple_of(x * assets + n * BLOCK, BLOCK), BLOCK)
            factor = steady[pl.ds(x * each + n, 1), :]
            mass[:, lanes] = (factor * mass[:, lanes].astype(f32)).astype(bf)
        return carry

    def chunk(c):
        return pl.ds(pl.multiple_of(c * chunk_rows, chunk_rows), chunk_rows)

    def move(step, c):
        return pltpu.make_async_remote_copy(
            src_ref=held.at[step - 1, chunk(c)],
            dst_ref=held.at[step, chunk(c)],
            send_sem=send_sem.at[step],
            recv_sem=recv_sem.at[step, c],
            device_id=target(step),
            device_id_type=MESH,
        )

    def last_move(y):
        rows = pl.ds(pl.multiple_of(y * cols, cols), cols)
        return pltpu.make_async_remote_copy(
            src_ref=held.at[STEPS - 1, rows],
            dst_ref=held.at[STEPS, rows],
            send_sem=send_sem.at[STEPS],
            recv_sem=last_sem.at[y],
            device_id=target(STEPS),
            device_id_type=MESH,
        )

    def across(src, dst, n, to):
        return pltpu.make_async_remote_copy(
            src_ref=src,
            dst_ref=dst,
            send_sem=tail_send.at[28 + n],
            recv_sem=tail_recv.at[28 + n],
            device_id=to,
            device_id_type=MESH,
        )

    early_moves = [
        across(rates.at[0], rates.at[1], 0, ahead),
        across(short.at[0], short.at[1], 1, hop_to),
        across(rates.at[0], rates.at[2], 2, behind),
        across(expect_in, lines.at[core], 3, other),
    ]
    lines_landed = across(expect_in, lines.at[1 - core], 3, other)
    raw_moves = [
        across(mass.at[:, part(n)], raw.at[:, part(n)], 4 + n, hop_to) for n in range(PARTS)
    ]
    for n in range(PARTS):
        loads[6 + n].wait()
        lax.fori_loop(n * types // PARTS, (n + 1) * types // PARTS, weigh, 0)
        if n == 0:
            pl.semaphore_wait(barrier, len(greeted))
        raw_moves[n].start()
    for copy in early_moves:
        copy.start()

    def beta_move(dh):
        return pltpu.make_async_remote_copy(
            src_ref=discount,
            dst_ref=betas.at[horizon],
            send_sem=tail_send.at[24 + dh],
            recv_sem=tail_recv.at[24 + dh],
            device_id=mate(dh),
            device_id_type=MESH,
        )

    def loop(body):
        lax.fori_loop(0, CHUNKS, lambda c, carry: (body(c), carry)[1], 0)

    for dh in (1, 2, 3):
        beta_move(dh).start()
    betas[horizon] = discount[...]

    spread_mix(trans, kron)
    locate(nodes, offsets, keys)
    for count, piece in land_pieces(mass, offsets, keys, kron, moved, landed, held.at[0]):
        lax.fori_loop(0, count, lambda n, carry, piece=piece: (piece(n), carry)[1], 0)
    loop(lambda c: move(1, c).start())

    early_moves[0].wait_recv()
    early_moves[2].wait_recv()
    diagonal = lax.broadcasted_iota(jnp.int32, (types, BLOCK), 0) == lax.broadcasted_iota(
        jnp.int32, (types, BLOCK), 1
    )
    mine = 1.0 - rates[0, 0:1, :] - rates[0, 1:2, :]
    for n, line in enumerate((mine, rates[1, 1:2, :], rates[2, 0:1, :])):
        upright = jnp.sum(jnp.where(diagonal, line, 0.0), axis=1, keepdims=True)
        weights[n] = jnp.broadcast_to(upright, (types, BLOCK))

    for copy in raw_moves:
        copy.wait_recv()
    early_moves[1].wait_recv()
    nodes[...] = short[1].astype(jnp.int32)
    locate(nodes, offsets, keys)
    pieces = land_pieces(raw, offsets, keys, kron, moved, landed, held.at[ONE_HOP])

    for step in range(1, STEPS - 1):

        def onward(c, step=step):
            move(step, c).wait_recv()
            move(step + 1, c).start()
            count, piece = pieces[step - 1]
            for n in range(count // CHUNKS):
                piece(c * (count // CHUNKS) + n)

        loop(onward)

    mirror = low + core * (3 - 2 * low)
    edge_low, edge_high = (3 - mirror) // 3, mirror // 3
    edge = edge_low + edge_high

    def multiply(late, y):
        same = 4 * (1 - edge_low) if late else 4 * edge_low
        prior = STEPS if late else 1
        after = 3 + 3 * edge if late else 6 - 3 * edge
        rows = pl.ds(pl.multiple_of(y * cols, cols), cols)
        total = None
        for n, slot in ((0, same), (1 + core, prior), (2 - core, after)):
            weight = jnp.concatenate([weights[n, pl.ds(y, 1), :]] * (assets // BLOCK), axis=1)
            term = held[slot, rows, :].astype(f32) * weight
            total = term if total is None else total + term
        lanes = pl.ds(pl.multiple_of(y * assets, assets), assets)
        right = jnp.concatenate([lines[0, :, lanes], lines[1, :, lanes]], axis=0)
        high = total.astype(bf)
        left = jnp.concatenate([high, (total - high.astype(f32)).astype(bf)], axis=0)
        both = lax.dot_general(left, right, NT, preferred_element_type=f32)
        flow[late] += both[:cols] + both[cols:]

    def beta_landed(dh):
        return pltpu.make_async_remote_copy(
            src_ref=discount,
            dst_ref=betas.at[(horizon + 4 - dh) % 4],
            send_sem=tail_send.at[24 + dh],
            recv_sem=tail_recv.at[24 + dh],
            device_id=mate(dh),
            device_id_type=MESH,
        )

    for dh in (1, 2, 3):
        beta_landed(dh).wait_recv()
    length = 4 * BLOCK
    hops = length.bit_length() - 1
    ids = lax.broadcasted_iota(jnp.int32, (2, length), 1)
    factor = jnp.concatenate([betas[h] for h in range(4)], axis=1)
    factor = jnp.broadcast_to(factor, (2, length))
    for n in range(hops):
        powers[n] = factor
        lagged = pltpu.roll(factor, length - 2**n, 1)
        factor = factor * jnp.where(ids < length - 2**n, lagged, 0.0)

    loads[5].wait()
    lines_landed.wait_recv()
    flow[...] = jnp.zeros_like(flow)

    def early(c):
        move(STEPS - 1, c).wait_recv()
        for i in range(chunk_types):
            last_move(c * chunk_types + i).start()
        for i in range(chunk_types):
            multiply(0, c * chunk_types + i)

    loop(early)

    def late(y, carry):
        last_move(y).wait_recv()
        multiply(1, y)
        return carry

    lax.fori_loop(0, types, late, 0)

    late_half = upper + (1 - edge_low) * (1 - 2 * upper)
    half[...] = jnp.zeros_like(half)
    for when, at in ((0, 1 - late_half), (1, late_half)):
        rows = pl.ds(pl.multiple_of((at * 2 + core) * cols, cols), cols)
        half[rows, : 2 * BLOCK] = flow[when]
    total = half[...]
    rows_at = lax.broadcasted_iota(jnp.int32, total.shape, 0)
    offset = 1
    while offset < 4 * cols:
        lagged = pltpu.roll(pltpu.roll(total, offset, 0), offset, 1)
        total = total + jnp.where(rows_at >= offset, lagged, 0.0)
        offset *= 2
    half[...] = total

    def plane_move(n, dx, dy):
        block = pl.ds(pl.multiple_of(plane_at(dx, dy) * 8, 8), 8)
        return pltpu.make_async_remote_copy(
            src_ref=half.at[block],
            dst_ref=from_plane.at[n],
            send_sem=tail_send.at[0],
            recv_sem=tail_recv.at[0],
            device_id=plane_peer(dx, dy),
            device_id_type=MESH,
        )

    def plane_all():
        return pltpu.make_async_remote_copy(
            src_ref=half.at[pl.ds(0, 8 * len(plane_turns))],
            dst_ref=from_plane,
            send_sem=tail_send.at[0],
            recv_sem=tail_recv.at[0],
            device_id=plane_peer(1, 0),
            device_id_type=MESH,
        )

    for n, (dx, dy) in enumerate(plane_turns):
        plane_move(n, dx, dy).start()

    for step in range(1, STEPS + 1):
        pltpu.make_async_remote_copy(
            src_ref=held.at[step - 1],
            dst_ref=held.at[step],
            send_sem=send_sem.at[step],
            recv_sem=recv_sem.at[1, 0],
            device_id=target(step),
            device_id_type=MESH,
        ).wait_send()
    for copy in early_moves + raw_moves:
        copy.wait_send()
    for k in (1, 2, 3):
        beta_move(k).wait_send()

    plane_all().wait_recv()
    parts = [half[pl.ds(pl.multiple_of(column * 8, 8), 8), :]]
    parts += [from_plane[n] for n in range(15)]
    while len(parts) > 1:
        parts = [a + b for a, b in zip(parts[::2], parts[1::2])]
    for q in range(4):
        pairs[q] = parts[0][2 * q : 2 * q + 2]
    here = z * 2 + core

    def line_move(dz, flip):
        return pltpu.make_async_remote_copy(
            src_ref=pairs.at[(low + dz) % 4],
            dst_ref=from_line.at[here],
            send_sem=tail_send.at[1],
            recv_sem=tail_recv.at[1],
            device_id=line_peer(dz, flip),
            device_id_type=MESH,
        )

    def line_all():
        return pltpu.make_async_remote_copy(
            src_ref=from_line.at[pl.ds(0, len(line_turns))],
            dst_ref=from_line.at[pl.ds(0, len(line_turns))],
            send_sem=tail_send.at[1],
            recv_sem=tail_recv.at[1],
            device_id=line_peer(1, 0),
            device_id_type=MESH,
        )

    for dz, flip in line_turns:
        line_move(dz, flip).start()
    from_line[here] = pairs[low]

    line_all().wait_recv()

    sums = []
    for n in range(2):
        parts = [from_line[8 * n + q] for q in range(8)]
        while len(parts) > 1:
            parts = [a + b for a, b in zip(parts[::2], parts[1::2])]
        sums.append(parts[0])
    jac = jnp.concatenate(
        [
            sums[0][:, : 2 * BLOCK],
            sums[1][:, :BLOCK] + sums[0][:, 2 * BLOCK :],
            sums[1][:, BLOCK : 2 * BLOCK],
        ],
        axis=1,
    )
    value = jac
    for n in range(hops):
        lagged = pltpu.roll(value, length - 2**n, 1)
        value = value + powers[n] * jnp.where(ids < length - 2**n, lagged, 0.0)
    wide[0] = jac
    wide[1] = value
    lanes = pl.ds(pl.multiple_of(horizon * BLOCK, BLOCK), BLOCK)
    out[...] = wide[:, :, lanes]
    plane_all().wait_send()
    line_all().wait_send()


def local(expect, steady_dist, policy_deriv, lottery_index, type_trans, migration, discount):
    types, assets = lottery_index.shape
    cols, states = policy_deriv.shape
    count = expect.shape[0]
    far = pl.BlockSpec(memory_space=pltpu.HBM)
    vmem = pl.BlockSpec(memory_space=pltpu.VMEM)
    both = pl.pallas_call(
        flow_kernel,
        out_shape=jax.ShapeDtypeStruct((2, 2, count), f32),
        in_specs=[far] * 7,
        out_specs=vmem,
        scratch_shapes=[
            pltpu.VMEM((2, count, states), bf),
            pltpu.VMEM((ONE_HOP + 1, types * cols, assets), bf),
            pltpu.VMEM((2, cols, 2 * count), f32),
            pltpu.VMEM((4 * cols, 3 * BLOCK), f32),
            pltpu.VMEM((4, 2, 3 * BLOCK), f32),
            pltpu.VMEM((15, 8, 3 * BLOCK), f32),
            pltpu.VMEM((16, 2, 3 * BLOCK), f32),
            pltpu.VMEM((4, 1, count), f32),
            pltpu.VMEM((2, 2, 4 * BLOCK), f32),
            pltpu.VMEM((9, 2, 4 * BLOCK), f32),
            pltpu.VMEM((cols, states), bf),
            pltpu.VMEM((cols, states), bf),
            pltpu.VMEM((states // BLOCK, BLOCK), f32),
            pltpu.VMEM((types, assets), jnp.int32),
            pltpu.VMEM((2, types, assets), jnp.int16),
            pltpu.VMEM((types, types), f32),
            pltpu.VMEM((2, types), bf),
            pltpu.VMEM((3, 8, BLOCK), f32),
            pltpu.VMEM((3, types, BLOCK), f32),
            pltpu.VMEM((assets // BLOCK, types, BLOCK), f32),
            pltpu.VMEM((4, types, BLOCK), f32),
            pltpu.VMEM((2 * types * 16, types * 16), bf),
            pltpu.VMEM((2, types, 32 * assets // BLOCK, 2 * BLOCK), bf),
            pltpu.VMEM((2, 2, types * 16, assets), bf),
            pltpu.VMEM((1, count), f32),
            pltpu.SemaphoreType.DMA((6 + PARTS,)),
            pltpu.SemaphoreType.DMA((STEPS + 1,)),
            pltpu.SemaphoreType.DMA((STEPS + 1, CHUNKS)),
            pltpu.SemaphoreType.DMA((types,)),
            pltpu.SemaphoreType.DMA((48 + PARTS,)),
            pltpu.SemaphoreType.DMA((48 + PARTS,)),
        ],
        compiler_params=pltpu.CompilerParams(
            collective_id=0, has_side_effects=True, vmem_limit_bytes=52 * 2**20
        ),
        name="flow",
    )(
        *[
            pltpu.with_memory_space_constraint(value, pltpu.HBM)
            for value in (
                expect,
                policy_deriv,
                steady_dist.reshape(-1, BLOCK),
                lottery_index,
                type_trans,
                migration.reshape(2, types),
                discount.reshape(1, count),
            )
        ]
    )
    return both[0], both[1]


def solution(mesh):
    return jax.shard_map(
        local,
        mesh=mesh,
        in_specs=(
            P("horizon", "state"),
            P("state"),
            P("horizon", "state"),
            P("state", None),
            P(),
            P("state", None, None),
            P("horizon"),
        ),
        out_specs=(P("state", "horizon"), P("state", "horizon")),
        check_vma=False,
    )
```
